32 devices in a mesh: branch: 4 (over y, x), attn: 8 (over z, core).
Axes of the slice: x: 2, y: 2, z: 4, core: 2. Of those that a mesh axis runs over, the one named last changes fastest.
Arguments:
- queries: bfloat16 [2, 32, 5120], P(None, ('branch', 'attn')), may hold values from -60 to 60
- new_kv: bfloat16 [2, 2, 32, 1024], P(None, None, ('branch', 'attn')), may hold values from -6 to 6
- tail_kv: bfloat16 [32, 63, 2, 1024], P(('branch', 'attn')), may hold values from -6 to 6
- pool_kv: bfloat16 [4, 288, 64, 2, 1024], P('branch', 'attn'), may hold values from -6 to 6
- resid: bfloat16 [2, 32, 5120], P(None, ('branch', 'attn')), may hold values from -0.3125 to 0.3125
- block_table: int32 [32, 144], P('branch'), may hold values from 0 to 287, as said below
- block_counts: int32 [32], P('branch'), may hold values from 36 to 144
- owner_map: int32 [4, 288], P('branch'), may hold values from 0 to 287, each once within a row
- fork_parent: int32 [4, 8], P('branch'), may hold values from 0 to 7, each once within a row
- norm_gain: bfloat16 [5120], replicated, may hold values from 0.5 to 1.5
- w_gate: bfloat16 [24576, 5120], P('attn', 'branch'), may hold values from -0.078125 to 0.078125
- w_up: bfloat16 [24576, 5120], P('attn', 'branch'), may hold values from -0.078125 to 0.078125
- w_down: bfloat16 [24576, 5120], P('attn', 'branch'), may hold values from -0.0390625 to 0.0390625
Outputs:
- layer_out: bfloat16 [2, 32, 5120], P(None, ('branch', 'attn'))
The draws below stay inside these ranges and needn't reach their ends.
Inputs may be any that keep to these rules, and one draw needn't show every extreme that they name: `block_table`: each branch's list names 144 distinct logical blocks of its group; only the first block_counts entries are its ancestors.
All inputs are finite; a program needn't handle non-finite values.
Results may differ from the reference program's by a relative error of at most 0.015.
Values may be sent and summed in bfloat16 or wider, within the bound.
A program may use at most 128 MiB of HBM per device.

```python
import jax
import jax.numpy as jnp
from jax import lax

D = 5120
H = 40
KVH = 8
HD = 128
FF = 24576
BLK = 64
KVD = 1024
TAIL = 63
GB = 8
BRANCHES = 32
GROUPS = 4
POOLB = 288
MAXB = 144


def draw_new_kv(key, part):
    sub = jax.random.fold_in(key, 11)
    return jnp.clip(jax.random.normal(sub, (2, 2, BRANCHES, KVD), jnp.float32), -6.0, 6.0).astype(jnp.bfloat16)


def draw_queries(key, part):
    sub = jax.random.fold_in(key, 23)
    fresh_key = jax.random.fold_in(key, 11)
    order = jnp.arange(BRANCHES, dtype=jnp.int32)
    picked = order % 16 == 0
    base = jnp.clip(jax.random.normal(sub, (2, BRANCHES, H * HD), jnp.float32), -6.0, 6.0)
    fresh = jnp.clip(jax.random.normal(fresh_key, (2, 2, BRANCHES, KVD), jnp.float32), -6.0, 6.0)[:, 0]
    strength = 6.0 + (order % 4).astype(jnp.float32)
    spread = jnp.broadcast_to(fresh.reshape(2, BRANCHES, KVH, 1, HD), (2, BRANCHES, KVH, H // KVH, HD)).reshape(2, BRANCHES, H * HD)
    signs = jnp.array([1.0, -1.0], jnp.float32)[:, None, None]
    aligned = spread * strength[None, :, None] * signs
    return jnp.where(picked[None, :, None], aligned, base).astype(jnp.bfloat16)


def draw_block_table(key, part):
    keys = jax.random.split(jax.random.fold_in(key, 31), BRANCHES)
    rows = jax.vmap(lambda single: jax.random.permutation(single, POOLB)[:MAXB])(keys)
    return rows.astype(jnp.int32)


def draw_block_counts(key, part):
    sub = jax.random.fold_in(key, 37)
    counts = jax.random.randint(sub, (BRANCHES,), MAXB // 4, MAXB + 1).astype(jnp.int32)
    counts = counts.at[0].set(MAXB)
    counts = counts.at[1].set(MAXB // 4)
    return counts


def steps_of(key, shape, cuts, low, top_value):
    def one(axis_at, blocks):
        draws = jax.random.uniform(jax.random.fold_in(jax.random.fold_in(key, 6), axis_at), (blocks,), jnp.float32, low / len(cuts), top_value / len(cuts))
        return jnp.repeat(jnp.exp(draws), shape[axis_at] // blocks).reshape((-1,) + (1,) * (len(shape) - axis_at - 1))

    gain = one(*cuts[0])
    for cut in cuts[1:]:
        gain = gain * one(*cut)
    return gain


def scatter_about(own_key, extent, scale, most, pieces=(), held_as=jnp.bfloat16):
    level = steps_of(own_key, extent, pieces, -0.22, 0.18) if pieces else 1.0
    values = jax.random.normal(own_key, extent, jnp.float32) * scale * level
    return jnp.minimum(jnp.maximum(values, -most), most).astype(held_as)


def setup_inputs(seed: int = 0) -> dict:
    streams_of = jax.random.split(jax.random.key(seed), 14)
    queries = draw_queries(jax.random.fold_in(streams_of[13], 71), 0)
    new_kv = draw_new_kv(jax.random.fold_in(streams_of[13], 71), 0)
    tail_kv = scatter_about(streams_of[2], (BRANCHES, TAIL, 2, KVD), 1.0, 6.0, ((0, 32),))
    pool_kv = scatter_about(streams_of[3], (GROUPS, POOLB, BLK, 2, KVD), 1.0, 6.0, ((0, 4), (1, 8)))
    resid = scatter_about(streams_of[4], (2, BRANCHES, D), 0.02, 0.3125, ((1, 32),))
    block_table = draw_block_table(jax.random.fold_in(streams_of[13], 71), 0)
    block_counts = draw_block_counts(jax.random.fold_in(streams_of[13], 71), 0)
    owner_map = jax.vmap(lambda own: jax.random.permutation(own, POOLB))(jax.random.split(streams_of[7], GROUPS)).reshape((GROUPS, POOLB)).astype(jnp.int32)
    fork_parent = jax.vmap(lambda own: jax.random.permutation(own, GB))(jax.random.split(streams_of[8], GROUPS)).reshape((GROUPS, GB)).astype(jnp.int32)
    norm_gain = jnp.clip(1.0 + 0.1 * jax.random.normal(streams_of[9], (D,), jnp.float32), 0.5, 1.5).astype(jnp.bfloat16)
    w_gate = scatter_about(streams_of[10], (FF, D), D ** -0.5, 0.078125, ((0, 8), (1, 4)))
    w_up = scatter_about(streams_of[11], (FF, D), D ** -0.5, 0.078125, ((0, 8), (1, 4)))
    w_down = scatter_about(streams_of[12], (FF, D), FF ** -0.5, 0.0390625, ((0, 8), (1, 4)))
    return {"queries": queries, "new_kv": new_kv, "tail_kv": tail_kv, "pool_kv": pool_kv, "resid": resid, "block_table": block_table, "block_counts": block_counts, "owner_map": owner_map, "fork_parent": fork_parent, "norm_gain": norm_gain, "w_gate": w_gate, "w_up": w_up, "w_down": w_down}


NEG = -1e+30
EPS = 1e-06

def block_partial(query, keys_vals, mask):
    nblk = keys_vals.shape[0]
    width = keys_vals.shape[1]
    rows = query.shape[0]
    group = H // KVH
    maxima, totals, accums = ([], [], [])
    for head in range(KVH):
        keys = keys_vals[:, :, 0, head * HD:(head + 1) * HD].reshape(nblk * width, HD).astype(jnp.float32)
        values = keys_vals[:, :, 1, head * HD:(head + 1) * HD].astype(jnp.float32)
        qpart = query[:, head * group:(head + 1) * group, :].astype(jnp.float32)
        scores = jnp.einsum('rhd,kd->rhk', qpart, keys) * HD ** (-0.5)
        scores = scores.reshape(rows, group, nblk, width)
        peak = lax.optimization_barrier(jnp.max(scores, axis=3))
        weights = jnp.exp(scores - peak[..., None]).astype(jnp.bfloat16).astype(jnp.float32)
        total = lax.optimization_barrier(jnp.sum(weights, axis=3))
        mixed = jnp.einsum('rhnl,nld->rhnd', weights, values)
        live = mask[:, None, :]
        peak = jnp.where(live, peak, NEG)
        top = lax.optimization_barrier(jnp.max(peak, axis=2))
        factor = jnp.where(live, jnp.exp(peak - top[..., None]), 0.0)
        maxima.append(top)
        totals.append(lax.optimization_barrier(jnp.sum(factor * total, axis=2)))
        accums.append(lax.optimization_barrier(jnp.sum(factor[..., None] * mixed, axis=2)))
    return (jnp.concatenate(maxima, axis=1), jnp.concatenate(totals, axis=1), jnp.concatenate(accums, axis=1))

def combine(first, second):
    top = jnp.maximum(first[0], second[0])
    left = jnp.exp(first[0] - top)
    right = jnp.exp(second[0] - top)
    return (top, left * first[1] + right * second[1], left[..., None] * first[2] + right[..., None] * second[2])

def finish(state):
    rows = state[2].shape[0]
    return (state[2] / state[1][..., None]).reshape(rows, H * HD).astype(jnp.bfloat16)

def reference(queries, new_kv, tail_kv, pool_kv, resid, block_table, block_counts, owner_map, fork_parent, norm_gain, w_gate, w_up, w_down):
    groups = pool_kv.shape[0]
    rows = BRANCHES // groups
    grouped_q = queries.reshape(2, groups, rows, H, HD).transpose(1, 0, 2, 3, 4)
    fresh_all = new_kv.reshape(2, 2, groups, rows, KVD).transpose(2, 0, 3, 1, 4)
    tails = tail_kv.reshape(groups, rows, TAIL, 2, KVD)
    tables = block_table.reshape(groups, rows, MAXB)
    counts = block_counts.reshape(groups, rows)

    def one_group(pack):
        query, fresh, tail, pool, table, count, owner, parent = pack
        live = jnp.arange(MAXB, dtype=jnp.int32)[None, :] < count[:, None]
        physical = owner[table]
        slot_ids = jnp.arange(POOLB, dtype=jnp.int32)
        pool_mask = jnp.any((physical[:, :, None] == slot_ids[None, None, :]) & live[:, :, None], axis=1)
        newest = jnp.concatenate([tail, fresh[0][:, None]], axis=1)
        diagonal = jnp.eye(rows, dtype=bool)
        first = combine(block_partial(query[0], pool, pool_mask), block_partial(query[0], newest, diagonal))
        parent_mask = parent[:, None] == jnp.arange(rows, dtype=jnp.int32)[None, :]
        second = combine(block_partial(query[1], pool, pool_mask), block_partial(query[1], newest, parent_mask))
        second = combine(second, block_partial(query[1], fresh[1][:, None], diagonal))
        return jnp.stack([finish(first), finish(second)])
    outs = lax.map(one_group, (grouped_q, fresh_all, tails, pool_kv, tables, counts, owner_map, fork_parent))
    attn = outs.transpose(1, 0, 2, 3).reshape(2, BRANCHES, D)
    hidden_x = resid.astype(jnp.float32) + attn.astype(jnp.float32)
    scale = lax.rsqrt(lax.optimization_barrier(jnp.mean(hidden_x * hidden_x, axis=-1, keepdims=True)) + EPS)
    normed = (hidden_x * scale * norm_gain.astype(jnp.float32)).astype(jnp.bfloat16).reshape(2 * BRANCHES, D)
    gate = jnp.dot(normed, w_gate.T, preferred_element_type=jnp.float32)
    upper = jnp.dot(normed, w_up.T, preferred_element_type=jnp.float32)
    inner = (jax.nn.silu(gate) * upper).astype(jnp.bfloat16)
    down = jnp.dot(inner, w_down, preferred_element_type=jnp.float32).reshape(2, BRANCHES, D)
    return (hidden_x + down).astype(jnp.bfloat16)
```

```python
import jax
import jax.numpy as jnp
from jax import lax
from jax.experimental import pallas as pl
from jax.experimental.pallas import tpu as pltpu
from jax.sharding import PartitionSpec as P

H = 40
KVH = 8
HD = 128
GRP = H // KVH
NEG = -1e30
EPS = 1e-06


def attend_kernel(q_ref, kv_ref, ex_ref, bias_ref, exbias_ref, acc_ref, m_ref, t_ref):
    q = q_ref[0]
    rows = bias_ref.shape[0]
    contract = (((1,), (1,)), ((), ()))

    def scored(keys, bias):
        s = lax.dot_general(q, keys, contract, preferred_element_type=jnp.float32)
        s = s.reshape(GRP, rows, s.shape[1]) * HD ** (-0.5) + bias[None]
        return s.reshape(GRP * rows, s.shape[2])

    s = scored(kv_ref[...], bias_ref[...])
    e = scored(ex_ref[...], exbias_ref[...])
    peak = jnp.maximum(
        jnp.max(s, axis=1, keepdims=True), jnp.max(e, axis=1, keepdims=True)
    )
    ps = jnp.exp(s - peak)
    pe = jnp.exp(e - peak)
    total = jnp.sum(ps, axis=1, keepdims=True) + jnp.sum(pe, axis=1, keepdims=True)
    ws = pltpu.roll(ps, 1, 1).astype(jnp.bfloat16)
    we = pltpu.roll(pe, 1, 1).astype(jnp.bfloat16)
    acc = jnp.dot(ws, kv_ref[...], preferred_element_type=jnp.float32)
    acc += jnp.dot(we, ex_ref[...], preferred_element_type=jnp.float32)
    acc_ref[0] = acc
    m_ref[0] = jnp.broadcast_to(peak, acc.shape)
    t_ref[0] = jnp.broadcast_to(total, acc.shape)


def attend(q, kv, ex, bias, exbias):
    n = q.shape[1]
    out = jax.ShapeDtypeStruct((KVH, n, HD), jnp.float32)
    head = pl.BlockSpec((1, n, HD), lambda h: (h, 0, 0))
    return pl.pallas_call(
        attend_kernel,
        grid=(KVH,),
        in_specs=[
            head,
            pl.BlockSpec((kv.shape[0], HD), lambda h: (0, h)),
            pl.BlockSpec((ex.shape[0], HD), lambda h: (0, h)),
            pl.BlockSpec(bias.shape, lambda h: (0, 0)),
            pl.BlockSpec(exbias.shape, lambda h: (0, 0)),
        ],
        out_specs=[head, head, head],
        out_shape=[out, out, out],
        compiler_params=pltpu.CompilerParams(vmem_limit_bytes=48 * 1024 * 1024),
    )(q, kv, ex, bias, exbias)


def partial_states(queries, new_kv, tail_kv, pool_kv, block_table, block_counts, owner_map, fork_parent):
    ranks = lax.axis_size("attn")
    mine = lax.axis_index("attn")
    nblk = pool_kv.shape[1]
    width = pool_kv.shape[2]
    kvd = pool_kv.shape[4]
    maxb = block_table.shape[1]
    pool_size = owner_map.shape[1]
    group_rows = 2 * ranks
    every_q = lax.all_gather(queries[:, 0], "attn", axis=0)
    q = (
        every_q.reshape(group_rows, KVH, GRP, HD)
        .transpose(1, 2, 0, 3)
        .reshape(KVH, GRP * group_rows, HD)
    )
    kv = pool_kv[0].reshape(nblk * width * 2, kvd)
    newest = jnp.concatenate([tail_kv[0], new_kv[0, :, 0][None]], axis=0)
    newest = newest.reshape(width * 2, kvd)
    second = jnp.pad(new_kv[1, :, 0], ((0, width * 2 - 2), (0, 0)))
    ex = jnp.concatenate([newest, second], axis=0)

    slots = mine * nblk + jnp.arange(nblk, dtype=jnp.int32)
    matches = owner_map[0][None, :] == slots[:, None]
    logical = jnp.sum(
        jnp.where(matches, jnp.arange(pool_size, dtype=jnp.int32)[None, :], 0), axis=1
    )
    live = jnp.arange(maxb, dtype=jnp.int32)[None, :] < block_counts[:, None]
    mask = jnp.any((block_table[:, :, None] == logical[None, None, :]) & live[:, :, None], axis=1)
    key_row = jnp.arange(width * 2, dtype=jnp.int32) % 2 == 0
    ok = mask[:, None, :, None] & key_row[None, None, None, :]
    ok = jnp.broadcast_to(ok, (ranks, 2, nblk, width * 2)).reshape(group_rows, nblk * width * 2)
    bias = jnp.where(ok, 0.0, NEG).astype(jnp.float32)
    own = jnp.arange(ranks, dtype=jnp.int32) == mine
    parent = fork_parent[0] == mine
    never = jnp.zeros_like(own)
    ex_new = jnp.stack([own, parent], axis=1).reshape(group_rows)
    ex_second = jnp.stack([never, own], axis=1).reshape(group_rows)
    first_row = jnp.arange(width * 2, dtype=jnp.int32) == 0
    exok = jnp.concatenate(
        [ex_new[:, None] & key_row[None], ex_second[:, None] & first_row[None]], axis=1
    )
    exbias = jnp.where(exok, 0.0, NEG).astype(jnp.float32)
    return attend(q, kv, ex, bias, exbias)


def feed(x, norm_gain, w_gate, w_up, w_down):
    scale = lax.rsqrt(jnp.mean(x * x, axis=-1, keepdims=True) + EPS)
    normed = (x * scale * norm_gain.astype(jnp.float32)).astype(jnp.bfloat16)
    rows = normed.shape[0]
    fanout = lax.axis_size("branch")
    ranks = lax.axis_size("attn")
    width = w_gate.shape[1]
    units = w_gate.shape[0]
    columns = lax.all_to_all(
        normed.reshape(rows, fanout, width), "branch", split_axis=1, concat_axis=0, tiled=True
    ).reshape(fanout * rows, width)
    gathered = lax.all_gather(columns, "attn", axis=0, tiled=True)
    ordered = (
        gathered.reshape(ranks, fanout, rows, width)
        .transpose(1, 0, 2, 3)
        .reshape(ranks * fanout * rows, width)
    )
    contract = (((1,), (1,)), ((), ()))
    gate = lax.dot_general(ordered, w_gate, contract, preferred_element_type=jnp.float32)
    upper = lax.dot_general(ordered, w_up, contract, preferred_element_type=jnp.float32)
    both = jnp.concatenate([gate, upper], axis=1).astype(jnp.bfloat16)
    parts = lax.all_to_all(
        both.reshape(fanout, ranks * rows, 2 * units), "branch", split_axis=0, concat_axis=0, tiled=True
    )
    summed = jnp.sum(parts.astype(jnp.float32), axis=0)
    share = (jax.nn.silu(summed[:, :units]) * summed[:, units:]).astype(jnp.bfloat16)
    inner = lax.all_gather(share, "branch", axis=0, tiled=True)
    flipped = (
        inner.reshape(fanout, ranks, rows, units)
        .transpose(1, 0, 2, 3)
        .reshape(ranks * fanout * rows, units)
    )
    down_part = lax.psum_scatter(
        jnp.dot(flipped, w_down, preferred_element_type=jnp.float32),
        "attn",
        scatter_dimension=0,
        tiled=True,
    )
    down = lax.all_to_all(down_part, "branch", split_axis=0, concat_axis=1, tiled=True)
    return (x + down).astype(jnp.bfloat16)


def local(
    queries,
    new_kv,
    tail_kv,
    pool_kv,
    resid,
    block_table,
    block_counts,
    owner_map,
    fork_parent,
    norm_gain,
    w_gate,
    w_up,
    w_down,
):
    ranks = lax.axis_size("attn")
    acc, peak, total = partial_states(
        queries, new_kv, tail_kv, pool_kv, block_table, block_counts, owner_map, fork_parent
    )

    def by_owner(array):
        w = array.shape[2]
        return (
            array.reshape(KVH, GRP, ranks, 2, w).transpose(2, 3, 0, 1, 4).reshape(ranks, 2, H, w)
        )

    packed = jnp.concatenate(
        [by_owner(acc), by_owner(peak[:, :, :1]), by_owner(total[:, :, :1])], axis=3
    ).reshape(ranks, 2 * H * (HD + 2))
    states = lax.all_to_all(packed, "attn", split_axis=0, concat_axis=0, tiled=True)
    states = states.reshape(ranks, 2, H, HD + 2)
    top = jnp.max(states[..., HD], axis=0)
    factor = jnp.exp(states[..., HD] - top)
    summed = jnp.sum(factor * states[..., HD + 1], axis=0)
    mixed = jnp.sum(factor[..., None] * states[..., :HD], axis=0)
    attn = (mixed / summed[..., None]).reshape(2, H * HD).astype(jnp.bfloat16)
    x = resid[:, 0].astype(jnp.float32) + attn.astype(jnp.float32)
    return feed(x, norm_gain, w_gate, w_up, w_down)[:, None]


def solution(mesh):
    return jax.shard_map(
        local,
        mesh=mesh,
        in_specs=(
            P(None, ("branch", "attn"), None),
            P(None, None, ("branch", "attn"), None),
            P(("branch", "attn"), None, None, None),
            P("branch", "attn", None, None, None),
            P(None, ("branch", "attn"), None),
            P("branch", None),
            P("branch"),
            P("branch", None),
            P("branch", None),
            P(),
            P("attn", "branch"),
            P("attn", "branch"),
            P("attn", "branch"),
        ),
        out_specs=P(None, ("branch", "attn"), None),
        check_vma=False,
    )
```

```python
import functools

import jax
import jax.numpy as jnp
from jax import lax
from jax.experimental import pallas as pl
from jax.experimental.pallas import tpu as pltpu
from jax.sharding import PartitionSpec as P

H = 40
KVH = 8
HD = 128
GRP = H // KVH
NEG = -1e30
EPS = 1e-06


def attend_kernel(q_ref, kv_ref, ex_ref, bias_ref, exbias_ref, acc_ref, m_ref, t_ref):
    q = q_ref[0]
    rows = bias_ref.shape[0]
    contract = (((1,), (1,)), ((), ()))

    def scored(keys, bias):
        s = lax.dot_general(q, keys, contract, preferred_element_type=jnp.float32)
        s = s.reshape(GRP, rows, s.shape[1]) * HD ** (-0.5) + bias[None]
        return s.reshape(GRP * rows, s.shape[2])

    s = scored(kv_ref[...], bias_ref[...])
    e = scored(ex_ref[...], exbias_ref[...])
    peak = jnp.maximum(
        jnp.max(s, axis=1, keepdims=True), jnp.max(e, axis=1, keepdims=True)
    )
    ps = jnp.exp(s - peak)
    pe = jnp.exp(e - peak)
    total = jnp.sum(ps, axis=1, keepdims=True) + jnp.sum(pe, axis=1, keepdims=True)
    ws = pltpu.roll(ps, 1, 1).astype(jnp.bfloat16)
    we = pltpu.roll(pe, 1, 1).astype(jnp.bfloat16)
    acc = jnp.dot(ws, kv_ref[...], preferred_element_type=jnp.float32)
    acc += jnp.dot(we, ex_ref[...], preferred_element_type=jnp.float32)
    acc_ref[0] = acc
    m_ref[0] = jnp.broadcast_to(peak, acc.shape)
    t_ref[0] = jnp.broadcast_to(total, acc.shape)


def attend(q, kv, ex, bias, exbias):
    n = q.shape[1]
    out = jax.ShapeDtypeStruct((KVH, n, HD), jnp.float32)
    head = pl.BlockSpec((1, n, HD), lambda h: (h, 0, 0))
    return pl.pallas_call(
        attend_kernel,
        grid=(KVH,),
        in_specs=[
            head,
            pl.BlockSpec((kv.shape[0], HD), lambda h: (0, h)),
            pl.BlockSpec((ex.shape[0], HD), lambda h: (0, h)),
            pl.BlockSpec(bias.shape, lambda h: (0, 0)),
            pl.BlockSpec(exbias.shape, lambda h: (0, 0)),
        ],
        out_specs=[head, head, head],
        out_shape=[out, out, out],
        compiler_params=pltpu.CompilerParams(vmem_limit_bytes=48 * 1024 * 1024),
    )(q, kv, ex, bias, exbias)


def partial_states(queries, new_kv, tail_kv, pool_kv, block_table, block_counts, owner_map, fork_parent):
    ranks = lax.axis_size("attn")
    mine = lax.axis_index("attn")
    nblk = pool_kv.shape[1]
    width = pool_kv.shape[2]
    kvd = pool_kv.shape[4]
    maxb = block_table.shape[1]
    pool_size = owner_map.shape[1]
    group_rows = 2 * ranks
    every_q = lax.all_gather(queries[:, 0], "attn", axis=0)
    q = (
        every_q.reshape(group_rows, KVH, GRP, HD)
        .transpose(1, 2, 0, 3)
        .reshape(KVH, GRP * group_rows, HD)
    )
    kv = pool_kv[0].reshape(nblk * width * 2, kvd)
    newest = jnp.concatenate([tail_kv[0], new_kv[0, :, 0][None]], axis=0)
    newest = newest.reshape(width * 2, kvd)
    second = jnp.pad(new_kv[1, :, 0], ((0, width * 2 - 2), (0, 0)))
    ex = jnp.concatenate([newest, second], axis=0)

    slots = mine * nblk + jnp.arange(nblk, dtype=jnp.int32)
    matches = owner_map[0][None, :] == slots[:, None]
    logical = jnp.sum(
        jnp.where(matches, jnp.arange(pool_size, dtype=jnp.int32)[None, :], 0), axis=1
    )
    live = jnp.arange(maxb, dtype=jnp.int32)[None, :] < block_counts[:, None]
    mask = jnp.any((block_table[:, :, None] == logical[None, None, :]) & live[:, :, None], axis=1)
    key_row = jnp.arange(width * 2, dtype=jnp.int32) % 2 == 0
    ok = mask[:, None, :, None] & key_row[None, None, None, :]
    ok = jnp.broadcast_to(ok, (ranks, 2, nblk, width * 2)).reshape(group_rows, nblk * width * 2)
    bias = jnp.where(ok, 0.0, NEG).astype(jnp.float32)
    own = jnp.arange(ranks, dtype=jnp.int32) == mine
    parent = fork_parent[0] == mine
    never = jnp.zeros_like(own)
    ex_new = jnp.stack([own, parent], axis=1).reshape(group_rows)
    ex_second = jnp.stack([never, own], axis=1).reshape(group_rows)
    first_row = jnp.arange(width * 2, dtype=jnp.int32) == 0
    exok = jnp.concatenate(
        [ex_new[:, None] & key_row[None], ex_second[:, None] & first_row[None]], axis=1
    )
    exbias = jnp.where(exok, 0.0, NEG).astype(jnp.float32)
    return attend(q, kv, ex, bias, exbias)


CHUNKS = 3


def feed_kernel(
    fanout, ranks, rows, nrm_ref, wg_hbm, wu_hbm, wd_hbm, out_ref,
    wg, wu, wd, cols, gath, xa, xb, part, precv, hid, acc, dperm, dsend, drecv, fsend, frecv,
    w_sem, a_send, a_recv, b_send, b_recv, p_send, p_recv, h_send, h_recv,
    d_send, d_recv, f_send, f_recv,
):
    me_b = lax.axis_index("branch")
    me_a = lax.axis_index("attn")
    uc = wg.shape[1]
    tokens = xa.shape[0]
    mesh_id = pl.DeviceIdType.MESH

    loads = []
    for c in range(CHUNKS):
        span = pl.ds(c * uc, uc)
        for k, (src, dst) in enumerate(((wg_hbm, wg), (wu_hbm, wu), (wd_hbm, wd))):
            loads.append((k, c, pltpu.make_async_copy(src.at[span], dst.at[c], w_sem.at[k, c])))
    loads.sort(key=lambda item: (item[0] == 2, item[1], item[0]))
    for _, _, load in loads:
        load.start()
    loads = {(k, c): load for k, c, load in loads}

    def at_branch(k):
        return (lax.rem(me_b + k, fanout), me_a)

    def at_attn(k):
        return (me_b, lax.rem(me_a + k, ranks))

    barrier = pltpu.get_barrier_semaphore()
    for k in range(1, fanout):
        pl.semaphore_signal(barrier, inc=1, device_id=at_branch(k), device_id_type=mesh_id)
    for k in range(1, ranks):
        pl.semaphore_signal(barrier, inc=1, device_id=at_attn(k), device_id_type=mesh_id)
    pl.semaphore_wait(barrier, fanout + ranks - 2)

    def send(src, dst, out_sem, in_sem, where):
        copy = pltpu.make_async_remote_copy(
            src_ref=src, dst_ref=dst, send_sem=out_sem, recv_sem=in_sem,
            device_id=where, device_id_type=mesh_id,
        )
        copy.start()
        return copy

    def finish(copies):
        for copy in copies:
            copy.wait_recv()

    sent = []
    stage = []
    for k in range(1, fanout):
        to = lax.rem(me_b + k, fanout)
        stage.append(send(nrm_ref.at[to], cols.at[me_b], a_send.at[k], a_recv.at[k], at_branch(k)))
    cols[me_b] = nrm_ref[me_b]
    finish(stage)
    sent += stage
    stage = []
    for k in range(1, ranks):
        stage.append(send(cols, gath.at[me_a], b_send.at[k], b_recv.at[k], at_attn(k)))
    gath[me_a] = cols[...]
    finish(stage)
    sent += stage
    for f in range(fanout):
        for a in range(ranks):
            at = (f * ranks + a) * rows
            xa[at : at + rows, :] = gath[a, f].astype(jnp.float32)
    xb[...] = xa[...].astype(jnp.bfloat16)

    contract = (((1,), (1,)), ((), ()))
    parts = []
    for c in range(CHUNKS):
        for k, weight in ((0, wg), (1, wu)):
            loads[k, c].wait()
            prod = lax.dot_general(
                xb[...], weight[c], contract, preferred_element_type=jnp.float32
            ).astype(jnp.bfloat16)
            part[c, :, :, k * uc : (k + 1) * uc] = prod.reshape(fanout, tokens // fanout, uc)
        stage = []
        for k in range(1, fanout):
            to = lax.rem(me_b + k, fanout)
            stage.append(
                send(part.at[c, to], precv.at[c, me_b], p_send.at[c, k], p_recv.at[c, k], at_branch(k))
            )
        parts.append(stage)
        sent += stage

    hidden = []
    for c in range(CHUNKS):
        finish(parts[c])
        summed = part[c, me_b].astype(jnp.float32)
        for k in range(1, fanout):
            summed += precv[c, lax.rem(me_b + k, fanout)].astype(jnp.float32)
        gate = summed[:, :uc]
        share = gate / (1.0 + jnp.exp(-gate)) * summed[:, uc:]
        hid[c, me_b] = share.astype(jnp.bfloat16)
        stage = []
        for k in range(1, fanout):
            stage.append(
                send(hid.at[c, me_b], hid.at[c, me_b], h_send.at[c, k], h_recv.at[c, k], at_branch(k))
            )
        hidden.append(stage)
        sent += stage

    for c in range(CHUNKS):
        loads[2, c].wait()
        finish(hidden[c])
        prod = jnp.dot(
            hid[c].reshape(tokens, uc), wd[c], preferred_element_type=jnp.float32
        )
        acc[...] = prod if c == 0 else acc[...] + prod

    for f in range(fanout):
        for a in range(ranks):
            at = (f * ranks + a) * rows
            dperm[a, f * rows : (f + 1) * rows, :] = acc[at : at + rows, :]
    dsend[...] = dperm[...].astype(jnp.bfloat16)
    stage = []
    for k in range(1, ranks):
        to = lax.rem(me_a + k, ranks)
        stage.append(send(dsend.at[to], drecv.at[me_a], d_send.at[k], d_recv.at[k], at_attn(k)))
    total = dperm[me_a]
    finish(stage)
    sent += stage
    for k in range(1, ranks):
        total += drecv[lax.rem(me_a + k, ranks)].astype(jnp.float32)
    for f in range(fanout):
        fsend[f] = total[f * rows : (f + 1) * rows, :]
    stage = []
    for k in range(1, fanout):
        to = lax.rem(me_b + k, fanout)
        stage.append(send(fsend.at[to], frecv.at[me_b], f_send.at[k], f_recv.at[k], at_branch(k)))
    frecv[me_b] = fsend[me_b]
    finish(stage)
    out_ref[...] = frecv[...]
    sent += stage
    for copy in sent:
        copy.wait_send()


def feed(x, norm_gain, w_gate, w_up, w_down):
    scale = lax.rsqrt(jnp.mean(x * x, axis=-1, keepdims=True) + EPS)
    normed = (x * scale * norm_gain.astype(jnp.float32)).astype(jnp.bfloat16)
    rows = normed.shape[0]
    fanout = lax.axis_size("branch")
    ranks = lax.axis_size("attn")
    units, width = w_gate.shape
    uc = units // CHUNKS
    tokens = fanout * ranks * rows
    sliced = normed.reshape(rows, fanout, width).transpose(1, 0, 2)
    vmem = pl.BlockSpec(memory_space=pltpu.VMEM)
    hbm = pl.BlockSpec(memory_space=pl.ANY)
    bf, f32 = jnp.bfloat16, jnp.float32
    dma = pltpu.SemaphoreType.DMA
    down = pl.pallas_call(
        functools.partial(feed_kernel, fanout, ranks, rows),
        in_specs=[vmem, hbm, hbm, hbm],
        out_specs=vmem,
        out_shape=jax.ShapeDtypeStruct((fanout, rows, width), f32),
        scratch_shapes=[
            pltpu.VMEM((CHUNKS, uc, width), bf),
            pltpu.VMEM((CHUNKS, uc, width), bf),
            pltpu.VMEM((CHUNKS, uc, width), bf),
            pltpu.VMEM((fanout, rows, width), bf),
            pltpu.VMEM((ranks, fanout, rows, width), bf),
            pltpu.VMEM((tokens, width), f32),
            pltpu.VMEM((tokens, width), bf),
            pltpu.VMEM((CHUNKS, fanout, tokens // fanout, 2 * uc), bf),
            pltpu.VMEM((CHUNKS, fanout, tokens // fanout, 2 * uc), bf),
            pltpu.VMEM((CHUNKS, fanout, tokens // fanout, uc), bf),
            pltpu.VMEM((tokens, width), f32),
            pltpu.VMEM((ranks, fanout * rows, width), f32),
            pltpu.VMEM((ranks, fanout * rows, width), bf),
            pltpu.VMEM((ranks, fanout * rows, width), bf),
            pltpu.VMEM((fanout, rows, width), f32),
            pltpu.VMEM((fanout, rows, width), f32),
            dma((3, CHUNKS)),
            dma((fanout,)),
            dma((fanout,)),
            dma((ranks,)),
            dma((ranks,)),
            dma((CHUNKS, fanout)),
            dma((CHUNKS, fanout)),
            dma((CHUNKS, fanout)),
            dma((CHUNKS, fanout)),
            dma((ranks,)),
            dma((ranks,)),
            dma((fanout,)),
            dma((fanout,)),
        ],
        compiler_params=pltpu.CompilerParams(
            collective_id=0, has_side_effects=True, vmem_limit_bytes=56 * 1024 * 1024
        ),
    )(sliced, w_gate, w_up, w_down)
    return (x + down.transpose(1, 0, 2).reshape(x.shape)).astype(jnp.bfloat16)


def local(
    queries,
    new_kv,
    tail_kv,
    pool_kv,
    resid,
    block_table,
    block_counts,
    owner_map,
    fork_parent,
    norm_gain,
    w_gate,
    w_up,
    w_down,
):
    ranks = lax.axis_size("attn")
    acc, peak, total = partial_states(
        queries, new_kv, tail_kv, pool_kv, block_table, block_counts, owner_map, fork_parent
    )

    def by_owner(array):
        w = array.shape[2]
        return (
            array.reshape(KVH, GRP, ranks, 2, w).transpose(2, 3, 0, 1, 4).reshape(ranks, 2, H, w)
        )

    packed = jnp.concatenate(
        [by_owner(acc), by_owner(peak[:, :, :1]), by_owner(total[:, :, :1])], axis=3
    ).reshape(ranks, 2 * H * (HD + 2))
    states = lax.all_to_all(packed, "attn", split_axis=0, concat_axis=0, tiled=True)
    states = states.reshape(ranks, 2, H, HD + 2)
    top = jnp.max(states[..., HD], axis=0)
    factor = jnp.exp(states[..., HD] - top)
    summed = jnp.sum(factor * states[..., HD + 1], axis=0)
    mixed = jnp.sum(factor[..., None] * states[..., :HD], axis=0)
    attn = (mixed / summed[..., None]).reshape(2, H * HD).astype(jnp.bfloat16)
    x = resid[:, 0].astype(jnp.float32) + attn.astype(jnp.float32)
    return feed(x, norm_gain, w_gate, w_up, w_down)[:, None]


def solution(mesh):
    return jax.shard_map(
        local,
        mesh=mesh,
        in_specs=(
            P(None, ("branch", "attn"), None),
            P(None, None, ("branch", "attn"), None),
            P(("branch", "attn"), None, None, None),
            P("branch", "attn", None, None, None),
            P(None, ("branch", "attn"), None),
            P("branch", None),
            P("branch"),
            P("branch", None),
            P("branch", None),
            P(),
            P("attn", "branch"),
            P("attn", "branch"),
            P("attn", "branch"),
        ),
        out_specs=P(None, ("branch", "attn"), None),
        check_vma=False,
    )
```

```python
import functools

import jax
import jax.numpy as jnp
from jax import lax
from jax.experimental import pallas as pl
from jax.experimental.pallas import tpu as pltpu
from jax.sharding import PartitionSpec as P

H = 40
KVH = 8
HD = 128
GRP = H // KVH
NEG = -1e30
EPS = 1e-06


def attend_kernel(q_ref, kv_ref, ex_ref, bias_ref, exbias_ref, acc_ref, m_ref, t_ref):
    q = q_ref[0]
    rows = bias_ref.shape[0]
    contract = (((1,), (1,)), ((), ()))

    def scored(keys, bias):
        s = lax.dot_general(q, keys, contract, preferred_element_type=jnp.float32)
        s = s.reshape(GRP, rows, s.shape[1]) * HD ** (-0.5) + bias[None]
        return s.reshape(GRP * rows, s.shape[2])

    s = scored(kv_ref[...], bias_ref[...])
    e = scored(ex_ref[...], exbias_ref[...])
    peak = jnp.maximum(
        jnp.max(s, axis=1, keepdims=True), jnp.max(e, axis=1, keepdims=True)
    )
    ps = jnp.exp(s - peak)
    pe = jnp.exp(e - peak)
    total = jnp.sum(ps, axis=1, keepdims=True) + jnp.sum(pe, axis=1, keepdims=True)
    ws = pltpu.roll(ps, 1, 1).astype(jnp.bfloat16)
    we = pltpu.roll(pe, 1, 1).astype(jnp.bfloat16)
    acc = jnp.dot(ws, kv_ref[...], preferred_element_type=jnp.float32)
    acc += jnp.dot(we, ex_ref[...], preferred_element_type=jnp.float32)
    acc_ref[0] = acc
    m_ref[0] = jnp.broadcast_to(peak, acc.shape)
    t_ref[0] = jnp.broadcast_to(total, acc.shape)


def attend(q, kv, ex, bias, exbias):
    n = q.shape[1]
    out = jax.ShapeDtypeStruct((KVH, n, HD), jnp.float32)
    head = pl.BlockSpec((1, n, HD), lambda h: (h, 0, 0))
    return pl.pallas_call(
        attend_kernel,
        grid=(KVH,),
        in_specs=[
            head,
            pl.BlockSpec((kv.shape[0], HD), lambda h: (0, h)),
            pl.BlockSpec((ex.shape[0], HD), lambda h: (0, h)),
            pl.BlockSpec(bias.shape, lambda h: (0, 0)),
            pl.BlockSpec(exbias.shape, lambda h: (0, 0)),
        ],
        out_specs=[head, head, head],
        out_shape=[out, out, out],
        compiler_params=pltpu.CompilerParams(vmem_limit_bytes=48 * 1024 * 1024),
    )(q, kv, ex, bias, exbias)


def partial_states(queries, new_kv, tail_kv, pool_kv, block_table, block_counts, owner_map, fork_parent):
    ranks = lax.axis_size("attn")
    mine = lax.axis_index("attn")
    nblk = pool_kv.shape[1]
    width = pool_kv.shape[2]
    kvd = pool_kv.shape[4]
    maxb = block_table.shape[1]
    pool_size = owner_map.shape[1]
    group_rows = 2 * ranks
    (every_q,) = swap([queries[:, 0]], True, 1)
    q = (
        every_q.reshape(group_rows, KVH, GRP, HD)
        .transpose(1, 2, 0, 3)
        .reshape(KVH, GRP * group_rows, HD)
    )
    kv = pool_kv[0].reshape(nblk * width * 2, kvd)
    newest = jnp.concatenate([tail_kv[0], new_kv[0, :, 0][None]], axis=0)
    newest = newest.reshape(width * 2, kvd)
    second = jnp.pad(new_kv[1, :, 0], ((0, width * 2 - 2), (0, 0)))
    ex = jnp.concatenate([newest, second], axis=0)

    slots = mine * nblk + jnp.arange(nblk, dtype=jnp.int32)
    matches = owner_map[0][None, :] == slots[:, None]
    logical = jnp.sum(
        jnp.where(matches, jnp.arange(pool_size, dtype=jnp.int32)[None, :], 0), axis=1
    )
    live = jnp.arange(maxb, dtype=jnp.int32)[None, :] < block_counts[:, None]
    mask = jnp.any((block_table[:, :, None] == logical[None, None, :]) & live[:, :, None], axis=1)
    key_row = jnp.arange(width * 2, dtype=jnp.int32) % 2 == 0
    ok = mask[:, None, :, None] & key_row[None, None, None, :]
    ok = jnp.broadcast_to(ok, (ranks, 2, nblk, width * 2)).reshape(group_rows, nblk * width * 2)
    bias = jnp.where(ok, 0.0, NEG).astype(jnp.float32)
    own = jnp.arange(ranks, dtype=jnp.int32) == mine
    parent = fork_parent[0] == mine
    never = jnp.zeros_like(own)
    ex_new = jnp.stack([own, parent], axis=1).reshape(group_rows)
    ex_second = jnp.stack([never, own], axis=1).reshape(group_rows)
    first_row = jnp.arange(width * 2, dtype=jnp.int32) == 0
    exok = jnp.concatenate(
        [ex_new[:, None] & key_row[None], ex_second[:, None] & first_row[None]], axis=1
    )
    exbias = jnp.where(exok, 0.0, NEG).astype(jnp.float32)
    return attend(q, kv, ex, bias, exbias)


def swap_kernel(ranks, gathers, *refs):
    count = (len(refs) - 2) // 3
    ins, outs, bufs = refs[:count], refs[count : 2 * count], refs[2 * count : 3 * count]
    out_sem, in_sem = refs[3 * count :]
    me_b = lax.axis_index("branch")
    me = lax.axis_index("attn")
    mesh_id = pl.DeviceIdType.MESH
    barrier = pltpu.get_barrier_semaphore()
    for k in range(1, ranks):
        pl.semaphore_signal(
            barrier, inc=1, device_id=(me_b, lax.rem(me + k, ranks)), device_id_type=mesh_id
        )
    pl.semaphore_wait(barrier, ranks - 1)
    copies = []
    for k in range(1, ranks):
        to = lax.rem(me + k, ranks)
        for i in range(count):
            copy = pltpu.make_async_remote_copy(
                src_ref=ins[i] if gathers else ins[i].at[to],
                dst_ref=bufs[i].at[me],
                send_sem=out_sem.at[i, k],
                recv_sem=in_sem.at[i, k],
                device_id=(me_b, to),
                device_id_type=mesh_id,
            )
            copy.start()
            copies.append(copy)
    for i in range(count):
        bufs[i][me] = ins[i][...] if gathers else ins[i][me]
    for copy in copies:
        copy.wait_recv()
    for i in range(count):
        outs[i][...] = bufs[i][...]
    for copy in copies:
        copy.wait_send()


def swap(arrays, gathers, collective_id):
    ranks = lax.axis_size("attn")
    shapes = [((ranks,) + a.shape if gathers else a.shape, a.dtype) for a in arrays]
    vmem = pl.BlockSpec(memory_space=pltpu.VMEM)
    return pl.pallas_call(
        functools.partial(swap_kernel, ranks, gathers),
        in_specs=[vmem] * len(arrays),
        out_specs=[vmem] * len(arrays),
        out_shape=[jax.ShapeDtypeStruct(*shape) for shape in shapes],
        scratch_shapes=[pltpu.VMEM(*shape) for shape in shapes]
        + [pltpu.SemaphoreType.DMA((len(arrays), ranks))] * 2,
        compiler_params=pltpu.CompilerParams(collective_id=collective_id, has_side_effects=True),
    )(*arrays)


CHUNKS = 3


def feed_kernel(
    fanout, ranks, rows, nrm_ref, wg_hbm, wu_hbm, wd_hbm, out_ref,
    wg, wu, wd, cols, gath, xa, xb, part, precv, hid, acc, dperm, dsend, drecv, fsend, frecv,
    w_sem, a_send, a_recv, b_send, b_recv, p_send, p_recv, h_send, h_recv,
    d_send, d_recv, f_send, f_recv,
):
    me_b = lax.axis_index("branch")
    me_a = lax.axis_index("attn")
    uc = wg.shape[1]
    tokens = xa.shape[0]
    mesh_id = pl.DeviceIdType.MESH

    loads = []
    for c in range(CHUNKS):
        span = pl.ds(c * uc, uc)
        for k, (src, dst) in enumerate(((wg_hbm, wg), (wu_hbm, wu), (wd_hbm, wd))):
            loads.append((k, c, pltpu.make_async_copy(src.at[span], dst.at[c], w_sem.at[k, c])))
    loads.sort(key=lambda item: (item[0] == 2, item[1], item[0]))
    for _, _, load in loads:
        load.start()
    loads = {(k, c): load for k, c, load in loads}

    def at_branch(k):
        return (lax.rem(me_b + k, fanout), me_a)

    def at_attn(k):
        return (me_b, lax.rem(me_a + k, ranks))

    barrier = pltpu.get_barrier_semaphore()
    for k in range(1, fanout):
        pl.semaphore_signal(barrier, inc=1, device_id=at_branch(k), device_id_type=mesh_id)
    for k in range(1, ranks):
        pl.semaphore_signal(barrier, inc=1, device_id=at_attn(k), device_id_type=mesh_id)
    pl.semaphore_wait(barrier, fanout + ranks - 2)

    def send(src, dst, out_sem, in_sem, where):
        copy = pltpu.make_async_remote_copy(
            src_ref=src, dst_ref=dst, send_sem=out_sem, recv_sem=in_sem,
            device_id=where, device_id_type=mesh_id,
        )
        copy.start()
        return copy

    def finish(copies):
        for copy in copies:
            copy.wait_recv()

    sent = []
    stage = []
    for k in range(1, fanout):
        to = lax.rem(me_b + k, fanout)
        stage.append(send(nrm_ref.at[to], cols.at[me_b], a_send.at[k], a_recv.at[k], at_branch(k)))
    cols[me_b] = nrm_ref[me_b]
    finish(stage)
    sent += stage
    stage = []
    for k in range(1, ranks):
        stage.append(send(cols, gath.at[me_a], b_send.at[k], b_recv.at[k], at_attn(k)))
    gath[me_a] = cols[...]
    finish(stage)
    sent += stage
    for f in range(fanout):
        for a in range(ranks):
            at = (f * ranks + a) * rows
            xa[at : at + rows, :] = gath[a, f].astype(jnp.float32)
    xb[...] = xa[...].astype(jnp.bfloat16)

    contract = (((1,), (1,)), ((), ()))
    parts = []
    for c in range(CHUNKS):
        for k, weight in ((0, wg), (1, wu)):
            loads[k, c].wait()
            prod = lax.dot_general(
                xb[...], weight[c], contract, preferred_element_type=jnp.float32
            ).astype(jnp.bfloat16)
            part[c, :, :, k * uc : (k + 1) * uc] = prod.reshape(fanout, tokens // fanout, uc)
        stage = []
        for k in range(1, fanout):
            to = lax.rem(me_b + k, fanout)
            stage.append(
                send(part.at[c, to], precv.at[c, me_b], p_send.at[c, k], p_recv.at[c, k], at_branch(k))
            )
        parts.append(stage)
        sent += stage

    hidden = []
    for c in range(CHUNKS):
        finish(parts[c])
        summed = part[c, me_b].astype(jnp.float32)
        for k in range(1, fanout):
            summed += precv[c, lax.rem(me_b + k, fanout)].astype(jnp.float32)
        gate = summed[:, :uc]
        share = gate / (1.0 + jnp.exp(-gate)) * summed[:, uc:]
        hid[c, me_b] = share.astype(jnp.bfloat16)
        stage = []
        for k in range(1, fanout):
            stage.append(
                send(hid.at[c, me_b], hid.at[c, me_b], h_send.at[c, k], h_recv.at[c, k], at_branch(k))
            )
        hidden.append(stage)
        sent += stage

    for c in range(CHUNKS):
        loads[2, c].wait()
        finish(hidden[c])
        prod = jnp.dot(
            hid[c].reshape(tokens, uc), wd[c], preferred_element_type=jnp.float32
        )
        acc[...] = prod if c == 0 else acc[...] + prod

    for f in range(fanout):
        for a in range(ranks):
            at = (f * ranks + a) * rows
            dperm[a, f * rows : (f + 1) * rows, :] = acc[at : at + rows, :]
    dsend[...] = dperm[...].astype(jnp.bfloat16)
    stage = []
    for k in range(1, ranks):
        to = lax.rem(me_a + k, ranks)
        stage.append(send(dsend.at[to], drecv.at[me_a], d_send.at[k], d_recv.at[k], at_attn(k)))
    total = dperm[me_a]
    finish(stage)
    sent += stage
    for k in range(1, ranks):
        total += drecv[lax.rem(me_a + k, ranks)].astype(jnp.float32)
    for f in range(fanout):
        fsend[f] = total[f * rows : (f + 1) * rows, :]
    stage = []
    for k in range(1, fanout):
        to = lax.rem(me_b + k, fanout)
        stage.append(send(fsend.at[to], frecv.at[me_b], f_send.at[k], f_recv.at[k], at_branch(k)))
    frecv[me_b] = fsend[me_b]
    finish(stage)
    out_ref[...] = frecv[...]
    sent += stage
    for copy in sent:
        copy.wait_send()


def feed(x, norm_gain, w_gate, w_up, w_down):
    scale = lax.rsqrt(jnp.mean(x * x, axis=-1, keepdims=True) + EPS)
    normed = (x * scale * norm_gain.astype(jnp.float32)).astype(jnp.bfloat16)
    rows = normed.shape[0]
    fanout = lax.axis_size("branch")
    ranks = lax.axis_size("attn")
    units, width = w_gate.shape
    uc = units // CHUNKS
    tokens = fanout * ranks * rows
    sliced = normed.reshape(rows, fanout, width).transpose(1, 0, 2)
    vmem = pl.BlockSpec(memory_space=pltpu.VMEM)
    hbm = pl.BlockSpec(memory_space=pl.ANY)
    bf, f32 = jnp.bfloat16, jnp.float32
    dma = pltpu.SemaphoreType.DMA
    down = pl.pallas_call(
        functools.partial(feed_kernel, fanout, ranks, rows),
        in_specs=[vmem, hbm, hbm, hbm],
        out_specs=vmem,
        out_shape=jax.ShapeDtypeStruct((fanout, rows, width), f32),
        scratch_shapes=[
            pltpu.VMEM((CHUNKS, uc, width), bf),
            pltpu.VMEM((CHUNKS, uc, width), bf),
            pltpu.VMEM((CHUNKS, uc, width), bf),
            pltpu.VMEM((fanout, rows, width), bf),
            pltpu.VMEM((ranks, fanout, rows, width), bf),
            pltpu.VMEM((tokens, width), f32),
            pltpu.VMEM((tokens, width), bf),
            pltpu.VMEM((CHUNKS, fanout, tokens // fanout, 2 * uc), bf),
            pltpu.VMEM((CHUNKS, fanout, tokens // fanout, 2 * uc), bf),
            pltpu.VMEM((CHUNKS, fanout, tokens // fanout, uc), bf),
            pltpu.VMEM((tokens, width), f32),
            pltpu.VMEM((ranks, fanout * rows, width), f32),
            pltpu.VMEM((ranks, fanout * rows, width), bf),
            pltpu.VMEM((ranks, fanout * rows, width), bf),
            pltpu.VMEM((fanout, rows, width), f32),
            pltpu.VMEM((fanout, rows, width), f32),
            dma((3, CHUNKS)),
            dma((fanout,)),
            dma((fanout,)),
            dma((ranks,)),
            dma((ranks,)),
            dma((CHUNKS, fanout)),
            dma((CHUNKS, fanout)),
            dma((CHUNKS, fanout)),
            dma((CHUNKS, fanout)),
            dma((ranks,)),
            dma((ranks,)),
            dma((fanout,)),
            dma((fanout,)),
        ],
        compiler_params=pltpu.CompilerParams(
            collective_id=0, has_side_effects=True, vmem_limit_bytes=56 * 1024 * 1024
        ),
    )(sliced, w_gate, w_up, w_down)
    return (x + down.transpose(1, 0, 2).reshape(x.shape)).astype(jnp.bfloat16)


def local(
    queries,
    new_kv,
    tail_kv,
    pool_kv,
    resid,
    block_table,
    block_counts,
    owner_map,
    fork_parent,
    norm_gain,
    w_gate,
    w_up,
    w_down,
):
    ranks = lax.axis_size("attn")
    acc, peak, total = partial_states(
        queries, new_kv, tail_kv, pool_kv, block_table, block_counts, owner_map, fork_parent
    )

    def by_owner(array):
        w = array.shape[2]
        return (
            array.reshape(KVH, GRP, ranks, 2, w).transpose(2, 3, 0, 1, 4).reshape(ranks, 2 * H, w)
        )

    stats = jnp.stack([by_owner(peak[:, :, :1])[..., 0], by_owner(total[:, :, :1])[..., 0]], axis=1)
    accs, stats = swap([by_owner(acc), stats], False, 2)
    top = jnp.max(stats[:, 0], axis=0)
    factor = jnp.exp(stats[:, 0] - top)
    summed = jnp.sum(factor * stats[:, 1], axis=0)
    mixed = jnp.sum(factor[..., None] * accs, axis=0)
    attn = (mixed / summed[..., None]).reshape(2, H * HD).astype(jnp.bfloat16)
    x = resid[:, 0].astype(jnp.float32) + attn.astype(jnp.float32)
    return feed(x, norm_gain, w_gate, w_up, w_down)[:, None]


def solution(mesh):
    return jax.shard_map(
        local,
        mesh=mesh,
        in_specs=(
            P(None, ("branch", "attn"), None),
            P(None, None, ("branch", "attn"), None),
            P(("branch", "attn"), None, None, None),
            P("branch", "attn", None, None, None),
            P(None, ("branch", "attn"), None),
            P("branch", None),
            P("branch"),
            P("branch", None),
            P("branch", None),
            P(),
            P("attn", "branch"),
            P("attn", "branch"),
            P("attn", "branch"),
        ),
        out_specs=P(None, ("branch", "attn"), None),
        check_vma=False,
    )
```

```python
import functools

import jax
import jax.numpy as jnp
from jax import lax
from jax.experimental import pallas as pl
from jax.experimental.pallas import tpu as pltpu
from jax.sharding import PartitionSpec as P

H = 40
KVH = 8
HD = 128
GRP = H // KVH
NEG = -1e30
EPS = 1e-06


def attend_kernel(q_ref, kv_ref, ex_ref, bias_ref, exbias_ref, acc_ref, m_ref, t_ref):
    q = q_ref[0]
    rows = bias_ref.shape[0]
    contract = (((1,), (1,)), ((), ()))

    def scored(keys, bias):
        s = lax.dot_general(q, keys, contract, preferred_element_type=jnp.float32)
        s = s.reshape(GRP, rows, s.shape[1]) * HD ** (-0.5) + bias[None]
        return s.reshape(GRP * rows, s.shape[2])

    s = scored(kv_ref[...], bias_ref[...])
    e = scored(ex_ref[...], exbias_ref[...])
    peak = jnp.maximum(
        jnp.max(s, axis=1, keepdims=True), jnp.max(e, axis=1, keepdims=True)
    )
    ps = jnp.exp(s - peak)
    pe = jnp.exp(e - peak)
    total = jnp.sum(ps, axis=1, keepdims=True) + jnp.sum(pe, axis=1, keepdims=True)
    ws = pltpu.roll(ps, 1, 1).astype(jnp.bfloat16)
    we = pltpu.roll(pe, 1, 1).astype(jnp.bfloat16)
    acc = jnp.dot(ws, kv_ref[...], preferred_element_type=jnp.float32)
    acc += jnp.dot(we, ex_ref[...], preferred_element_type=jnp.float32)
    acc_ref[0] = acc
    m_ref[0] = jnp.broadcast_to(peak, acc.shape)
    t_ref[0] = jnp.broadcast_to(total, acc.shape)


def attend(q, kv, ex, bias, exbias):
    n = q.shape[1]
    out = jax.ShapeDtypeStruct((KVH, n, HD), jnp.float32)
    head = pl.BlockSpec((1, n, HD), lambda h: (h, 0, 0))
    return pl.pallas_call(
        attend_kernel,
        grid=(KVH,),
        in_specs=[
            head,
            pl.BlockSpec((kv.shape[0], HD), lambda h: (0, h)),
            pl.BlockSpec((ex.shape[0], HD), lambda h: (0, h)),
            pl.BlockSpec(bias.shape, lambda h: (0, 0)),
            pl.BlockSpec(exbias.shape, lambda h: (0, 0)),
        ],
        out_specs=[head, head, head],
        out_shape=[out, out, out],
        compiler_params=pltpu.CompilerParams(vmem_limit_bytes=48 * 1024 * 1024),
    )(q, kv, ex, bias, exbias)


def partial_states(queries, new_kv, tail_kv, pool_kv, block_table, block_counts, owner_map, fork_parent):
    ranks = lax.axis_size("attn")
    mine = lax.axis_index("attn")
    nblk = pool_kv.shape[1]
    width = pool_kv.shape[2]
    kvd = pool_kv.shape[4]
    maxb = block_table.shape[1]
    pool_size = owner_map.shape[1]
    group_rows = 2 * ranks
    pieces = [queries[:, 0]] + [
        lax.ppermute(queries[:, 0], "attn", [(a, (a + k) % ranks) for a in range(ranks)])
        for k in range(1, ranks)
    ]
    backward = jnp.stack((pieces[::-1]) * 2)
    every_q = lax.dynamic_slice_in_dim(backward, ranks - 1 - mine, ranks, 0)
    q = (
        every_q.reshape(group_rows, KVH, GRP, HD)
        .transpose(1, 2, 0, 3)
        .reshape(KVH, GRP * group_rows, HD)
    )
    kv = pool_kv[0].reshape(nblk * width * 2, kvd)
    newest = jnp.concatenate([tail_kv[0], new_kv[0, :, 0][None]], axis=0)
    newest = newest.reshape(width * 2, kvd)
    second = jnp.pad(new_kv[1, :, 0], ((0, width * 2 - 2), (0, 0)))
    ex = jnp.concatenate([newest, second], axis=0)

    slots = mine * nblk + jnp.arange(nblk, dtype=jnp.int32)
    matches = owner_map[0][None, :] == slots[:, None]
    logical = jnp.sum(
        jnp.where(matches, jnp.arange(pool_size, dtype=jnp.int32)[None, :], 0), axis=1
    )
    live = jnp.arange(maxb, dtype=jnp.int32)[None, :] < block_counts[:, None]
    mask = jnp.any((block_table[:, :, None] == logical[None, None, :]) & live[:, :, None], axis=1)
    key_row = jnp.arange(width * 2, dtype=jnp.int32) % 2 == 0
    ok = mask[:, None, :, None] & key_row[None, None, None, :]
    ok = jnp.broadcast_to(ok, (ranks, 2, nblk, width * 2)).reshape(group_rows, nblk * width * 2)
    bias = jnp.where(ok, 0.0, NEG).astype(jnp.float32)
    own = jnp.arange(ranks, dtype=jnp.int32) == mine
    parent = fork_parent[0] == mine
    never = jnp.zeros_like(own)
    ex_new = jnp.stack([own, parent], axis=1).reshape(group_rows)
    ex_second = jnp.stack([never, own], axis=1).reshape(group_rows)
    first_row = jnp.arange(width * 2, dtype=jnp.int32) == 0
    exok = jnp.concatenate(
        [ex_new[:, None] & key_row[None], ex_second[:, None] & first_row[None]], axis=1
    )
    exbias = jnp.where(exok, 0.0, NEG).astype(jnp.float32)
    return attend(q, kv, ex, bias, exbias)


def swap_kernel(ranks, gathers, *refs):
    count = (len(refs) - 2) // 3
    ins, outs, bufs = refs[:count], refs[count : 2 * count], refs[2 * count : 3 * count]
    out_sem, in_sem = refs[3 * count :]
    me_b = lax.axis_index("branch")
    me = lax.axis_index("attn")
    mesh_id = pl.DeviceIdType.MESH
    barrier = pltpu.get_barrier_semaphore()
    for k in range(1, ranks):
        pl.semaphore_signal(
            barrier, inc=1, device_id=(me_b, lax.rem(me + k, ranks)), device_id_type=mesh_id
        )
    pl.semaphore_wait(barrier, ranks - 1)
    copies = []
    for k in range(1, ranks):
        to = lax.rem(me + k, ranks)
        for i in range(count):
            copy = pltpu.make_async_remote_copy(
                src_ref=ins[i] if gathers else ins[i].at[to],
                dst_ref=bufs[i].at[me],
                send_sem=out_sem.at[i, k],
                recv_sem=in_sem.at[i, k],
                device_id=(me_b, to),
                device_id_type=mesh_id,
            )
            copy.start()
            copies.append(copy)
    for i in range(count):
        bufs[i][me] = ins[i][...] if gathers else ins[i][me]
    for copy in copies:
        copy.wait_recv()
    for i in range(count):
        outs[i][...] = bufs[i][...]
    for copy in copies:
        copy.wait_send()


def swap(arrays, gathers, collective_id):
    ranks = lax.axis_size("attn")
    shapes = [((ranks,) + a.shape if gathers else a.shape, a.dtype) for a in arrays]
    vmem = pl.BlockSpec(memory_space=pltpu.VMEM)
    return pl.pallas_call(
        functools.partial(swap_kernel, ranks, gathers),
        in_specs=[vmem] * len(arrays),
        out_specs=[vmem] * len(arrays),
        out_shape=[jax.ShapeDtypeStruct(*shape) for shape in shapes],
        scratch_shapes=[pltpu.VMEM(*shape) for shape in shapes]
        + [pltpu.SemaphoreType.DMA((len(arrays), ranks))] * 2,
        compiler_params=pltpu.CompilerParams(collective_id=collective_id, has_side_effects=True),
    )(*arrays)


CHUNKS = 3


def feed_kernel(
    fanout, ranks, rows, nrm_ref, wg_hbm, wu_hbm, wd_hbm, out_ref,
    wg, wu, wd, cols, gath, xa, xb, part, precv, hid, acc, dperm, dsend, drecv, fsend, frecv,
    w_sem, a_send, a_recv, b_send, b_recv, p_send, p_recv, h_send, h_recv,
    d_send, d_recv, f_send, f_recv,
):
    me_b = lax.axis_index("branch")
    me_a = lax.axis_index("attn")
    uc = wg.shape[1]
    tokens = xa.shape[0]
    mesh_id = pl.DeviceIdType.MESH

    loads = []
    for c in range(CHUNKS):
        span = pl.ds(c * uc, uc)
        for k, (src, dst) in enumerate(((wg_hbm, wg), (wu_hbm, wu), (wd_hbm, wd))):
            loads.append((k, c, pltpu.make_async_copy(src.at[span], dst.at[c], w_sem.at[k, c])))
    loads.sort(key=lambda item: (item[0] == 2, item[1], item[0]))
    for _, _, load in loads:
        load.start()
    loads = {(k, c): load for k, c, load in loads}

    def at_branch(k):
        return (lax.rem(me_b + k, fanout), me_a)

    def at_attn(k):
        return (me_b, lax.rem(me_a + k, ranks))

    barrier = pltpu.get_barrier_semaphore()
    for k in range(1, fanout):
        pl.semaphore_signal(barrier, inc=1, device_id=at_branch(k), device_id_type=mesh_id)
    for k in range(1, ranks):
        pl.semaphore_signal(barrier, inc=1, device_id=at_attn(k), device_id_type=mesh_id)
    pl.semaphore_wait(barrier, fanout + ranks - 2)

    def send(src, dst, out_sem, in_sem, where):
        copy = pltpu.make_async_remote_copy(
            src_ref=src, dst_ref=dst, send_sem=out_sem, recv_sem=in_sem,
            device_id=where, device_id_type=mesh_id,
        )
        copy.start()
        return copy

    def finish(copies):
        for copy in copies:
            copy.wait_recv()

    sent = []
    stage = []
    for k in range(1, fanout):
        to = lax.rem(me_b + k, fanout)
        stage.append(send(nrm_ref.at[to], cols.at[me_b], a_send.at[k], a_recv.at[k], at_branch(k)))
    cols[me_b] = nrm_ref[me_b]
    finish(stage)
    sent += stage
    stage = []
    for k in range(1, ranks):
        stage.append(send(cols, gath.at[me_a], b_send.at[k], b_recv.at[k], at_attn(k)))
    gath[me_a] = cols[...]
    finish(stage)
    sent += stage
    for f in range(fanout):
        for a in range(ranks):
            at = (f * ranks + a) * rows
            xa[at : at + rows, :] = gath[a, f].astype(jnp.float32)
    xb[...] = xa[...].astype(jnp.bfloat16)

    contract = (((1,), (1,)), ((), ()))
    parts = []
    for c in range(CHUNKS):
        for k, weight in ((0, wg), (1, wu)):
            loads[k, c].wait()
            prod = lax.dot_general(
                xb[...], weight[c], contract, preferred_element_type=jnp.float32
            ).astype(jnp.bfloat16)
            part[c, :, :, k * uc : (k + 1) * uc] = prod.reshape(fanout, tokens // fanout, uc)
        stage = []
        for k in range(1, fanout):
            to = lax.rem(me_b + k, fanout)
            stage.append(
                send(part.at[c, to], precv.at[c, me_b], p_send.at[c, k], p_recv.at[c, k], at_branch(k))
            )
        parts.append(stage)
        sent += stage

    hidden = []
    for c in range(CHUNKS):
        finish(parts[c])
        summed = part[c, me_b].astype(jnp.float32)
        for k in range(1, fanout):
            summed += precv[c, lax.rem(me_b + k, fanout)].astype(jnp.float32)
        gate = summed[:, :uc]
        share = gate / (1.0 + jnp.exp(-gate)) * summed[:, uc:]
        hid[c, me_b] = share.astype(jnp.bfloat16)
        stage = []
        for k in range(1, fanout):
            stage.append(
                send(hid.at[c, me_b], hid.at[c, me_b], h_send.at[c, k], h_recv.at[c, k], at_branch(k))
            )
        hidden.append(stage)
        sent += stage

    for c in range(CHUNKS):
        loads[2, c].wait()
        finish(hidden[c])
        prod = jnp.dot(
            hid[c].reshape(tokens, uc), wd[c], preferred_element_type=jnp.float32
        )
        acc[...] = prod if c == 0 else acc[...] + prod

    for f in range(fanout):
        for a in range(ranks):
            at = (f * ranks + a) * rows
            dperm[a, f * rows : (f + 1) * rows, :] = acc[at : at + rows, :]
    dsend[...] = dperm[...].astype(jnp.bfloat16)
    stage = []
    for k in range(1, ranks):
        to = lax.rem(me_a + k, ranks)
        stage.append(send(dsend.at[to], drecv.at[me_a], d_send.at[k], d_recv.at[k], at_attn(k)))
    total = dperm[me_a]
    finish(stage)
    sent += stage
    for k in range(1, ranks):
        total += drecv[lax.rem(me_a + k, ranks)].astype(jnp.float32)
    for f in range(fanout):
        fsend[f] = total[f * rows : (f + 1) * rows, :]
    stage = []
    for k in range(1, fanout):
        to = lax.rem(me_b + k, fanout)
        stage.append(send(fsend.at[to], frecv.at[me_b], f_send.at[k], f_recv.at[k], at_branch(k)))
    frecv[me_b] = fsend[me_b]
    finish(stage)
    out_ref[...] = frecv[...]
    sent += stage
    for copy in sent:
        copy.wait_send()


def feed(x, norm_gain, w_gate, w_up, w_down):
    scale = lax.rsqrt(jnp.mean(x * x, axis=-1, keepdims=True) + EPS)
    normed = (x * scale * norm_gain.astype(jnp.float32)).astype(jnp.bfloat16)
    rows = normed.shape[0]
    fanout = lax.axis_size("branch")
    ranks = lax.axis_size("attn")
    units, width = w_gate.shape
    uc = units // CHUNKS
    tokens = fanout * ranks * rows
    sliced = normed.reshape(rows, fanout, width).transpose(1, 0, 2)
    vmem = pl.BlockSpec(memory_space=pltpu.VMEM)
    hbm = pl.BlockSpec(memory_space=pl.ANY)
    bf, f32 = jnp.bfloat16, jnp.float32
    dma = pltpu.SemaphoreType.DMA
    down = pl.pallas_call(
        functools.partial(feed_kernel, fanout, ranks, rows),
        in_specs=[vmem, hbm, hbm, hbm],
        out_specs=vmem,
        out_shape=jax.ShapeDtypeStruct((fanout, rows, width), f32),
        scratch_shapes=[
            pltpu.VMEM((CHUNKS, uc, width), bf),
            pltpu.VMEM((CHUNKS, uc, width), bf),
            pltpu.VMEM((CHUNKS, uc, width), bf),
            pltpu.VMEM((fanout, rows, width), bf),
            pltpu.VMEM((ranks, fanout, rows, width), bf),
            pltpu.VMEM((tokens, width), f32),
            pltpu.VMEM((tokens, width), bf),
            pltpu.VMEM((CHUNKS, fanout, tokens // fanout, 2 * uc), bf),
            pltpu.VMEM((CHUNKS, fanout, tokens // fanout, 2 * uc), bf),
            pltpu.VMEM((CHUNKS, fanout, tokens // fanout, uc), bf),
            pltpu.VMEM((tokens, width), f32),
            pltpu.VMEM((ranks, fanout * rows, width), f32),
            pltpu.VMEM((ranks, fanout * rows, width), bf),
            pltpu.VMEM((ranks, fanout * rows, width), bf),
            pltpu.VMEM((fanout, rows, width), f32),
            pltpu.VMEM((fanout, rows, width), f32),
            dma((3, CHUNKS)),
            dma((fanout,)),
            dma((fanout,)),
            dma((ranks,)),
            dma((ranks,)),
            dma((CHUNKS, fanout)),
            dma((CHUNKS, fanout)),
            dma((CHUNKS, fanout)),
            dma((CHUNKS, fanout)),
            dma((ranks,)),
            dma((ranks,)),
            dma((fanout,)),
            dma((fanout,)),
        ],
        compiler_params=pltpu.CompilerParams(
            collective_id=0, has_side_effects=True, vmem_limit_bytes=56 * 1024 * 1024
        ),
    )(sliced, w_gate, w_up, w_down)
    return (x + down.transpose(1, 0, 2).reshape(x.shape)).astype(jnp.bfloat16)


def local(
    queries,
    new_kv,
    tail_kv,
    pool_kv,
    resid,
    block_table,
    block_counts,
    owner_map,
    fork_parent,
    norm_gain,
    w_gate,
    w_up,
    w_down,
):
    ranks = lax.axis_size("attn")
    acc, peak, total = partial_states(
        queries, new_kv, tail_kv, pool_kv, block_table, block_counts, owner_map, fork_parent
    )

    def by_owner(array):
        w = array.shape[2]
        return (
            array.reshape(KVH, GRP, ranks, 2, w).transpose(2, 3, 0, 1, 4).reshape(ranks, 2 * H, w)
        )

    stats = jnp.stack([by_owner(peak[:, :, :1])[..., 0], by_owner(total[:, :, :1])[..., 0]], axis=1)
    accs, stats = swap([by_owner(acc), stats], False, 2)
    top = jnp.max(stats[:, 0], axis=0)
    factor = jnp.exp(stats[:, 0] - top)
    summed = jnp.sum(factor * stats[:, 1], axis=0)
    mixed = jnp.sum(factor[..., None] * accs, axis=0)
    attn = (mixed / summed[..., None]).reshape(2, H * HD).astype(jnp.bfloat16)
    x = resid[:, 0].astype(jnp.float32) + attn.astype(jnp.float32)
    return feed(x, norm_gain, w_gate, w_up, w_down)[:, None]


def solution(mesh):
    return jax.shard_map(
        local,
        mesh=mesh,
        in_specs=(
            P(None, ("branch", "attn"), None),
            P(None, None, ("branch", "attn"), None),
            P(("branch", "attn"), None, None, None),
            P("branch", "attn", None, None, None),
            P(None, ("branch", "attn"), None),
            P("branch", None),
            P("branch"),
            P("branch", None),
            P("branch", None),
            P(),
            P("attn", "branch"),
            P("attn", "branch"),
            P("attn", "branch"),
        ),
        out_specs=P(None, ("branch", "attn"), None),
        check_vma=False,
    )
```
